512 devices in a mesh: feat: 128 (over y, x, z_lo, core), layer: 4 (over z_hi).
Axes of the slice: x: 4, y: 8, z: 8 (z_hi: 4, z_lo: 2; z = z_hi * 2 + z_lo), core: 2. Of those that a mesh axis runs over, the one named last changes fastest.
Arguments:
- residual_in: bfloat16 [4, 384, 2304], P('layer', 'feat'), as said below
- enc_weight: bfloat16 [4, 2304, 8192], P('layer', None, 'feat'), as said below
- thresholds: int32 [4, 8192], P('layer', 'feat'), may hold values from -2016 to 7341, as said below
- dec_weight: bfloat16 [4, 4, 8192, 2304], P(None, 'layer', 'feat'), may hold values from -0.03125 to 0.03125
- target: bfloat16 [4, 384, 2304], P('layer', 'feat')
Outputs:
- loss_value: float32 [], replicated
- reconstruction: bfloat16 [4, 384, 2304], P('layer', 'feat')
- dec_grad: bfloat16 [4, 4, 8192, 2304], P(None, 'layer', 'feat')
- enc_grad: bfloat16 [4, 2304, 8192], P('layer', None, 'feat')
The draws below stay inside these ranges and needn't reach their ends.
Inputs may be any that keep to these rules, and one draw needn't show every extreme that they name: `residual_in`: every entry is a multiple of 1/8. `enc_weight`: every entry is a multiple of 1/256. `thresholds`: whole numbers.
All inputs are finite; a program needn't handle non-finite values.
Results may differ from the reference program's by a relative error of at most 0.007.
Values may be sent and summed in bfloat16 or wider, within the bound.
A program may use at most 64 MiB of HBM per device.

```python
import jax
import jax.numpy as jnp

D = 2304
FEAT = 8192
NSRC = 4
NTGT = 4
TOKENS = 384


def column_factor():
    return 1 + 3 * jnp.arange(FEAT, dtype=jnp.int32) // FEAT


def draw_residual_in(key, part):
    levels = jax.random.randint(key, (NSRC, TOKENS, D), -16, 17)
    return (levels.astype(jnp.float32) / 8.0).astype(jnp.bfloat16)


def draw_enc_weight(key, part):
    levels = jax.random.randint(key, (NSRC, D, FEAT), -8, 9)
    scaled = levels * column_factor()[None, None, :]
    return (scaled.astype(jnp.float32) / 256.0).astype(jnp.bfloat16)


def draw_thresholds(key, part):
    spread = min(D // 8, 48)
    levels = jax.random.randint(key, (NSRC, FEAT), -14 * spread, 51 * spread)
    levels = levels.at[0, FEAT - 1].set(51 * spread - 1)
    levels = levels.at[0, FEAT - 2].set(-14 * spread)
    return (levels * column_factor()[None, :]).astype(jnp.int32)


def draw_target(key, part):
    row_index = jnp.arange(TOKENS, dtype=jnp.float32)
    row_scale = 1.0 + 3.0 * row_index / TOKENS
    values = jax.random.normal(key, (NTGT, TOKENS, D))
    return (values * row_scale[None, :, None]).astype(jnp.bfloat16)


def level_of(key, dims, cuts, low, high):
    factor_of = 1.0
    for dim, shards_of in cuts:
        heights = jax.random.uniform(jax.random.fold_in(jax.random.fold_in(key, 6), dim), (shards_of,), jnp.float32, low / len(cuts), high / len(cuts))
        factor_of = factor_of * jnp.repeat(jnp.exp(heights), dims[dim] // shards_of).reshape((-1,) + (1,) * (len(dims) - 1 - dim))
    return factor_of


def scatter_about(own_key, shape, scale, limit, shards=(), kind=jnp.bfloat16):
    array = jax.random.normal(own_key, shape, jnp.float32) * scale
    if len(shards) > 0:
        array = level_of(own_key, shape, shards, -0.22, 0.18) * array
    return jnp.clip(array, min=-limit, max=limit).astype(kind)


def setup_inputs(seed: int = 0) -> dict:
    streams_of = jax.random.split(jax.random.key(seed), 6)
    return {
        "residual_in": draw_residual_in(jax.random.fold_in(streams_of[5], 71), 0),
        "enc_weight": draw_enc_weight(jax.random.fold_in(streams_of[5], 71), 0),
        "thresholds": draw_thresholds(jax.random.fold_in(streams_of[5], 71), 0),
        "dec_weight": scatter_about(streams_of[3], (NSRC, NTGT, FEAT, D), (NSRC * FEAT) ** -0.5, 0.03125, ((1, 4), (2, 128))),
        "target": draw_target(jax.random.fold_in(streams_of[5], 71), 0),
    }


ERROR_SCALE = 32.0
PENALTY_WEIGHT = 4.0


def reference(residual_in, enc_weight, thresholds, dec_weight, target):
    jump_level = (thresholds.astype(jnp.float32) + 0.5) / 2048.0
    preactivation = jnp.stack([jnp.dot(residual_in[source], enc_weight[source], preferred_element_type=jnp.float32) for source in range(NSRC)])
    active_mask = preactivation > jump_level[:, None, :]
    feature_activations = jnp.where(active_mask, preactivation, 0.0).astype(jnp.bfloat16)
    magnitude = jnp.mean(jnp.abs(feature_activations.astype(jnp.float32)), axis=1)
    penalty = jnp.sum(magnitude * magnitude)
    outputs = []
    for layer_out in range(NTGT):
        summed = jnp.dot(feature_activations[0], dec_weight[0, layer_out], preferred_element_type=jnp.float32)
        for source in range(1, NSRC):
            summed = summed + jnp.dot(feature_activations[source], dec_weight[source, layer_out], preferred_element_type=jnp.float32)
        outputs.append(summed)
    recon = jnp.stack(outputs)
    error_rows = recon - target.astype(jnp.float32)
    squares = jnp.sum(error_rows * error_rows)
    loss_value = (squares + 2.0 * ERROR_SCALE * PENALTY_WEIGHT * penalty) / (NTGT * TOKENS * D)
    grad = (error_rows / ERROR_SCALE).astype(jnp.bfloat16)
    dec_grad = jnp.stack([jnp.stack([jnp.dot(feature_activations[source].T, grad[layer_out], preferred_element_type=jnp.float32).astype(jnp.bfloat16) for layer_out in range(NTGT)]) for source in range(NSRC)])
    act_list = []
    for source in range(NSRC):
        summed = jnp.dot(grad[0], dec_weight[source, 0].T, preferred_element_type=jnp.float32)
        for layer_out in range(1, NTGT):
            summed = summed + jnp.dot(grad[layer_out], dec_weight[source, layer_out].T, preferred_element_type=jnp.float32)
        act_list.append(summed)
    activation_gradient = jnp.stack(act_list)
    sparsity_gradient = 2.0 * PENALTY_WEIGHT * magnitude[:, None, :] * jnp.sign(feature_activations.astype(jnp.float32)) / TOKENS
    preactivation_gradient = jnp.where(active_mask, activation_gradient + sparsity_gradient, 0.0).astype(jnp.bfloat16)
    enc_grad = jnp.stack([jnp.dot(residual_in[source].T, preactivation_gradient[source], preferred_element_type=jnp.float32).astype(jnp.bfloat16) for source in range(NSRC)])
    return (loss_value, recon.astype(jnp.bfloat16), dec_grad, enc_grad)
```

```python
import functools

import jax
import jax.numpy as jnp
from jax import lax
from jax.experimental import pallas as pl
from jax.experimental.pallas import tpu as pltpu
from jax.sharding import PartitionSpec as P

ERROR_SCALE = 32.0
PENALTY_WEIGHT = 4.0
MESH = pl.DeviceIdType.MESH
PLANE = 8
CORES = 2
NCH = 6
BF = jnp.bfloat16
F32 = jnp.float32


def nt(a, b):
    return lax.dot_general(a, b, (((1,), (1,)), ((), ())), preferred_element_type=F32)


def nn(a, b):
    return lax.dot_general(a, b, (((1,), (0,)), ((), ())), preferred_element_type=F32)


def kernel(
    dims,
    x_in, enc_in, th_in, dec_in, tgt_in,
    loss_out, rec_out, dg_out, eg_out,
    st, gs, gown, tmp, xb, gb, xp, gp,
    encb, decb, cutb, msum, pre, acts, act_t, act_o,
    part, rs_s, rs_r, so, si,
    agf, ags, agr, pgt, pgo, dgv, egv,
    sc_p, sc_y, sc_l, sc_c,
    loc_sem, d2d_s, d2d_r, pl_s, pl_r, ring_s, ring_r, lay_s, lay_r, ys_s, ys_r,
):
    ny, nl, r, d, f = dims
    half = ny // 2
    cw = d // NCH
    rows = PLANE * r
    tokens = ny * rows * CORES
    feat = lax.axis_index("feat")
    zh = lax.axis_index("layer")
    c = lax.rem(feat, CORES)
    p = lax.rem(feat // CORES, PLANE)
    y = feat // (CORES * PLANE)

    def dev(yy, pp, cc, ll):
        return (yy * (PLANE * CORES) + pp * CORES + cc, ll)

    def ymod(v):
        return lax.rem(v + 2 * ny, ny)

    def pmod(v):
        return lax.rem(v + PLANE, PLANE)

    def lmod(v):
        return lax.rem(v + nl, nl)

    def remote(src, dst, ss, rs, device):
        return pltpu.make_async_remote_copy(
            src_ref=src, dst_ref=dst, send_sem=ss, recv_sem=rs, device_id=device, device_id_type=MESH
        )

    partner = dev(y, p, 1 - c, zh)

    enc_cp = pltpu.make_async_copy(enc_in, encb.at[c], loc_sem.at[0])
    enc_cp.start()
    dec_cp = pltpu.make_async_copy(dec_in, decb.at[:, c], loc_sem.at[1])
    dec_cp.start()
    x_cp = pltpu.make_async_copy(x_in, st.at[p], loc_sem.at[2])
    x_cp.start()

    cut = (th_in[...].astype(F32) + 0.5) / 2048.0
    zero = jnp.zeros_like(cut)
    cutb[0] = jnp.where(c == 0, jnp.concatenate([cut, zero], 1), jnp.concatenate([zero, cut], 1))

    barrier = pltpu.get_barrier_semaphore()
    peers = [dev(y, pmod(p + j), c, zh) for j in range(1, PLANE)]
    peers += [dev(ymod(y + j), p, c, zh) for j in range(1, ny)]
    peers += [dev(y, p, c, lmod(zh + j)) for j in range(1, nl)]
    peers += [partner]
    for peer in peers:
        pl.semaphore_signal(barrier, inc=1, device_id=peer, device_id_type=MESH)
    pl.semaphore_wait(barrier, len(peers))

    pending = []

    def plane_start(which, source, dest):
        out = []
        for j in range(1, PLANE):
            q = pmod(p + j)
            cp = remote(source(q), dest.at[p], pl_s.at[which, j - 1], pl_r.at[which, j - 1], dev(y, q, c, zh))
            cp.start()
            out.append(cp)
        pending.extend(out)
        return out

    def d2d_start(which, source, dest):
        cp = remote(source, dest, d2d_s.at[which], d2d_r.at[which], partner)
        cp.start()
        pending.append(cp)
        return cp

    def repack(staged, block):
        for i in range(PLANE):
            tmp[r * i : r * (i + 1), :] = staged[i].astype(F32)
        block[y] = tmp[...].astype(BF)

    def ring_copy(base, buf, way, s, k):
        blk = ymod(y - s) if way == 0 else ymod(y + s)
        to = ymod(y + 1) if way == 0 else ymod(y - 1)
        piece = buf.at[blk, :, pl.ds(k * cw, cw)]
        return remote(piece, piece, ring_s.at[base, way, s, k], ring_r.at[base, way, s, k], dev(to, p, c, zh))

    def lanes(way, s):
        if s < half - 1:
            return range(NCH)
        return range(NCH // 2) if way == 0 else range(NCH // 2, NCH)

    def ring_gather(base, buf):
        sent = []
        for k in range(NCH):
            for way in (0, 1):
                if k in lanes(way, 0):
                    cp = ring_copy(base, buf, way, 0, k)
                    cp.start()
                    sent.append(cp)
        for s in range(half):
            for k in range(NCH):
                for way in (0, 1):
                    if k in lanes(way, s):
                        ring_copy(base, buf, way, s, k).wait_recv()
                        if s + 1 < half and k in lanes(way, s + 1):
                            cp = ring_copy(base, buf, way, s + 1, k)
                            cp.start()
                            sent.append(cp)
        pending.extend(sent)

    xs = plane_start(0, lambda q: x_in, st)
    enc_d = d2d_start(0, enc_in, encb.at[c])
    cut_d = d2d_start(2, cutb.at[0], cutb.at[1])
    dec_d = d2d_start(1, dec_in, decb.at[:, c])
    x_cp.wait()
    for cp in xs:
        cp.wait_recv()
    repack(st, xb)
    ring_gather(0, xb)
    x_d = d2d_start(4, xb, xp)

    enc_cp.wait()
    enc_d.wait_recv()
    cut_d.wait_recv()
    xv = xb[...].reshape(ny * rows, d)
    ev = encb[...].reshape(CORES * f, d)
    pa = nt(xv, ev)
    pre[...] = pa
    level = cutb[0] + cutb[1]
    act = jnp.where(pa > level, pa, 0.0).astype(BF)
    acts[zh] = act

    def layer_start(which, source, dest):
        out = []
        for j in range(1, nl):
            l = lmod(zh + j)
            cp = remote(source(l), dest.at[zh], lay_s.at[which, j - 1], lay_r.at[which, j - 1], dev(y, p, c, l))
            cp.start()
            out.append(cp)
        pending.extend(out)
        return out

    al = layer_start(0, lambda l: acts.at[zh], acts)
    msum[0] = jnp.sum(jnp.abs(act.astype(F32)), axis=0, keepdims=True)
    mag_d = d2d_start(3, msum.at[0], msum.at[1])
    dec_cp.wait()
    dec_d.wait_recv()
    for cp in al:
        cp.wait_recv()

    av = jnp.concatenate([acts[s] for s in range(nl)], axis=1)
    part[...] = nn(av, decb[...].reshape(nl * CORES * f, d)).reshape(ny, rows, d)

    def rs_lanes(way, s):
        return lanes(way, half - 1 - s)

    def rs_copy(way, s, k):
        to = ymod(y + 1) if way == 0 else ymod(y - 1)
        cols = pl.ds(k * cw, cw)
        return remote(
            rs_s.at[way, s, :, cols], rs_r.at[way, s, :, cols],
            ring_s.at[2, way, s, k], ring_r.at[2, way, s, k], dev(to, p, c, zh),
        )

    def rs_step(way, s, k):
        blk = ymod(y + half - s) if way == 0 else ymod(y - half + s)
        cols = pl.ds(k * cw, cw)
        value = part[blk, :, cols]
        if s > 0 and k in rs_lanes(way, s - 1):
            rs_copy(way, s - 1, k).wait_recv()
            value = value + rs_r[way, s - 1, :, cols].astype(F32)
        rs_s[way, s, :, cols] = value.astype(BF)
        cp = rs_copy(way, s, k)
        cp.start()
        pending.append(cp)

    for s in range(half):
        for k in range(NCH):
            for way in (0, 1):
                if k in rs_lanes(way, s):
                    rs_step(way, s, k)

    for s in range(nl):
        act_t[s] = jnp.transpose(acts[s].astype(F32)).astype(BF)
    act_d = d2d_start(5, act_t.at[:, pl.ds(pl.multiple_of((1 - c) * f, f), f)], act_o)

    for k in range(NCH):
        cols = pl.ds(k * cw, cw)
        for way in (0, 1):
            rs_copy(way, half - 1, k).wait_recv()
        tmp[:, cols] = part[y, :, cols] + rs_r[0, half - 1, :, cols].astype(F32) + rs_r[1, half - 1, :, cols].astype(F32)
    for i in range(PLANE):
        so[i] = tmp[r * i : r * (i + 1), :].astype(BF)
    ps = plane_start(1, lambda q: so.at[q], si)
    si[p] = so[p]
    for cp in ps:
        cp.wait_recv()
    recon = si[0].astype(F32)
    for i in range(1, PLANE):
        recon = recon + si[i].astype(F32)
    rec_out[...] = recon.astype(BF)
    error = recon - tgt_in[...].astype(F32)
    gown[...] = (error * (1.0 / ERROR_SCALE)).astype(BF)
    gs[p] = gown[...]
    gsd = plane_start(2, lambda q: gown, gs)
    mag_d.wait_recv()
    magnitude = (msum[0] + msum[1]) * (1.0 / tokens)
    penalty = jnp.sum(magnitude * magnitude)
    scalar = jnp.sum(error * error) + (2.0 * ERROR_SCALE * PENALTY_WEIGHT / CORES) * penalty
    sc_p[p] = jnp.full((1, 128), scalar, F32)
    scp = plane_start(3, lambda q: sc_p.at[p], sc_p)
    for cp in gsd:
        cp.wait_recv()
    repack(gs, gb)
    ring_gather(1, gb)
    g_d = d2d_start(6, gb, gp)

    gv = gb[...].reshape(ny * rows, d)
    for s in range(nl):
        ag = nt(gv, decb[s].reshape(CORES * f, d))
        agf[s] = ag
        ags[s] = ag.astype(BF)
    agl = layer_start(1, lambda l: ags.at[l], agr)

    def fold(slots, n):
        total = slots[0]
        for i in range(1, n):
            total = total + slots[i]
        return total

    for cp in scp:
        cp.wait_recv()
    sc_y[y] = fold(sc_p, PLANE)
    scy = []
    for j in range(1, ny):
        to = ymod(y + j)
        cp = remote(sc_y.at[y], sc_y.at[y], ys_s.at[j - 1], ys_r.at[j - 1], dev(to, p, c, zh))
        cp.start()
        scy.append(cp)
    pending.extend(scy)

    act_d.wait_recv()
    g_d.wait_recv()
    go = gp[...].reshape(ny * rows, d)
    own = pl.ds(pl.multiple_of(c * f, f), f)
    lhs = jnp.concatenate([act_t[s, own, :] for s in range(nl)], axis=0)
    lho = jnp.concatenate([act_o[s] for s in range(nl)], axis=0)
    dgv[...] = (nn(lhs, gv) + nn(lho, go)).astype(BF).reshape(nl, f, d)
    dg_cp = pltpu.make_async_copy(dgv, dg_out, loc_sem.at[3])
    dg_cp.start()

    for cp in scy:
        cp.wait_recv()
    sc_l[zh] = fold(sc_y, ny)
    scl = layer_start(2, lambda l: sc_l.at[zh], sc_l)

    for cp in agl:
        cp.wait_recv()
    act_grad = agf[zh]
    for j in range(1, nl):
        act_grad = act_grad + agr[lmod(zh + j)].astype(F32)
    pv = pre[...]
    fire = pv > level
    sign = jnp.where(fire & (pv > 0.0), 1.0, 0.0) - jnp.where(fire & (pv < 0.0), 1.0, 0.0)
    sparsity = (2.0 * PENALTY_WEIGHT) * magnitude * sign / float(tokens)
    pg = jnp.where(fire, act_grad + sparsity, 0.0)
    pgt[...] = jnp.transpose(pg).astype(BF)
    pg_d = d2d_start(7, pgt.at[pl.ds(pl.multiple_of((1 - c) * f, f), f)], pgo)
    for cp in scl:
        cp.wait_recv()
    sc_c[c] = fold(sc_l, nl)
    sc_d = d2d_start(8, sc_c.at[c], sc_c.at[c])
    x_d.wait_recv()
    eg = nn(pgt[own, :], xb[...].reshape(ny * rows, d))
    pg_d.wait_recv()
    eg = eg + nn(pgo[...], xp[...].reshape(ny * rows, d))
    egv[...] = eg.astype(BF)
    eg_cp = pltpu.make_async_copy(egv, eg_out, loc_sem.at[4])
    eg_cp.start()
    sc_d.wait_recv()
    loss_out[...] = fold(sc_c, CORES) * (1.0 / (nl * tokens * d))
    for cp in pending:
        cp.wait_send()
    dg_cp.wait()
    eg_cp.wait()


def solution(mesh):
    nl = mesh.shape["layer"]
    ny = mesh.shape["feat"] // (PLANE * CORES)

    def body(residual_in, enc_weight, thresholds, dec_weight, target):
        r, d = residual_in.shape[1:]
        f = enc_weight.shape[2]
        rows = PLANE * r
        half = ny // 2
        t = ny * rows
        any_spec = pl.BlockSpec(memory_space=pl.ANY)
        vm = pl.BlockSpec(memory_space=pltpu.VMEM)
        V = pltpu.VMEM
        dma = pltpu.SemaphoreType.DMA
        loss, rec, dg, eg = pl.pallas_call(
            functools.partial(kernel, (ny, nl, r, d, f)),
            out_shape=(
                jax.ShapeDtypeStruct((1, 128), F32),
                jax.ShapeDtypeStruct((r, d), BF),
                jax.ShapeDtypeStruct((nl, f, d), BF),
                jax.ShapeDtypeStruct((f, d), BF),
            ),
            in_specs=[any_spec, any_spec, vm, any_spec, vm],
            out_specs=(vm, vm, any_spec, any_spec),
            scratch_shapes=[
                V((PLANE, r, d), BF), V((PLANE, r, d), BF), V((r, d), BF), V((rows, d), F32),
                V((ny, rows, d), BF), V((ny, rows, d), BF), V((ny, rows, d), BF), V((ny, rows, d), BF),
                V((CORES, f, d), BF), V((nl, CORES, f, d), BF), V((2, 1, CORES * f), F32), V((2, 1, CORES * f), F32),
                V((t, CORES * f), F32), V((nl, t, CORES * f), BF), V((nl, CORES * f, t), BF), V((nl, f, t), BF),
                V((ny, rows, d), F32), V((2, half, rows, d), BF), V((2, half, rows, d), BF),
                V((PLANE, r, d), BF), V((PLANE, r, d), BF),
                V((nl, t, CORES * f), F32), V((nl, t, CORES * f), BF), V((nl, t, CORES * f), BF),
                V((CORES * f, t), BF), V((f, t), BF), V((nl, f, d), BF), V((f, d), BF),
                V((PLANE, 1, 128), F32), V((ny, 1, 128), F32), V((nl, 1, 128), F32), V((CORES, 1, 128), F32),
                dma((5,)), dma((9,)), dma((9,)), dma((4, PLANE - 1)), dma((4, PLANE - 1)),
                dma((3, 2, half, NCH)), dma((3, 2, half, NCH)), dma((3, nl - 1)), dma((3, nl - 1)),
                dma((ny - 1,)), dma((ny - 1,)),
            ],
            compiler_params=pltpu.CompilerParams(
                collective_id=0, has_side_effects=True, vmem_limit_bytes=56 * 1024 * 1024
            ),
            name="step",
        )(
            residual_in[0],
            jnp.swapaxes(enc_weight[0], 0, 1),
            thresholds,
            dec_weight[:, 0],
            target[0],
        )
        return loss[0, 0], rec[None], dg[:, None], jnp.swapaxes(eg, 0, 1)[None]

    return jax.shard_map(
        body,
        mesh=mesh,
        in_specs=(
            P("layer", "feat", None),
            P("layer", None, "feat"),
            P("layer", "feat"),
            P(None, "layer", "feat", None),
            P("layer", "feat", None),
        ),
        out_specs=(
            P(),
            P("layer", "feat", None),
            P(None, "layer", "feat", None),
            P("layer", None, "feat"),
        ),
        check_vma=False,
    )
```

```python
import functools

import jax
import jax.numpy as jnp
import numpy as np
from jax import lax
from jax.experimental import pallas as pl
from jax.experimental.pallas import tpu as pltpu
from jax.sharding import PartitionSpec as P

ERROR_SCALE = 32.0
PENALTY_WEIGHT = 4.0
MESH = pl.DeviceIdType.MESH
PLANE = 8
CORES = 2
PARTS = 3
BF = jnp.bfloat16
F32 = jnp.float32


def nt(a, b):
    return lax.dot_general(a, b, (((1,), (1,)), ((), ())), preferred_element_type=F32)


def nn(a, b):
    return lax.dot_general(a, b, (((1,), (0,)), ((), ())), preferred_element_type=F32)


def kernel(
    dims,
    x_in, enc_in, th_in, dec_in, tgt_in, perm_in,
    loss_out, rec_out, dg_out, eg_out,
    st_a, st_b, gs_a, gs_b, gown, tmp_a, tmp_b, xb, gb, xp, gp, xq, gq,
    thr, tgt, encb, decb, cutb, msum, pre, acts, act_t, act_o, perm,
    part_a, part_b, rs_a, rs_b, rr_a, rr_b, so_a, so_b, si_a, si_b,
    agf, ags, agr, pgt, pgo,
    sc_p, sc_y, sc_l, sc_c,
    loc_sem, d2d_s, d2d_r, pl_s, pl_r, ys_s, ys_r, lay_s, lay_r,
):
    ny, nl, r, d, f = dims
    wa = d // PARTS
    wb = d - wa
    ca, cb = pl.ds(0, wa), pl.ds(wa, wb)
    rows = PLANE * r
    rows_b = ny * r
    tokens = ny * rows * CORES
    feat = lax.axis_index("feat")
    zh = lax.axis_index("layer")
    c = lax.rem(feat, CORES)
    p = lax.rem(feat // CORES, PLANE)
    y = feat // (CORES * PLANE)

    def dev(yy, pp, cc, ll):
        return (yy * (PLANE * CORES) + pp * CORES + cc, ll)

    def ymod(v):
        return lax.rem(v + 2 * ny, ny)

    def pmod(v):
        return lax.rem(v + PLANE, PLANE)

    def lmod(v):
        return lax.rem(v + nl, nl)

    def remote(src, dst, ss, rs, device):
        return pltpu.make_async_remote_copy(
            src_ref=src, dst_ref=dst, send_sem=ss, recv_sem=rs, device_id=device, device_id_type=MESH
        )

    partner = dev(y, p, 1 - c, zh)

    enc_cp = pltpu.make_async_copy(enc_in, encb.at[c], loc_sem.at[0])
    enc_cp.start()
    dec_cp = pltpu.make_async_copy(dec_in, decb.at[:, c], loc_sem.at[1])
    dec_cp.start()
    xa_cp = pltpu.make_async_copy(x_in.at[:, ca], st_a.at[p], loc_sem.at[2])
    xa_cp.start()
    xb_cp = pltpu.make_async_copy(x_in.at[:, cb], st_b.at[y], loc_sem.at[3])
    xb_cp.start()
    perm_cp = pltpu.make_async_copy(perm_in, perm, loc_sem.at[4])
    perm_cp.start()
    th_cp = pltpu.make_async_copy(th_in, thr, loc_sem.at[5])
    th_cp.start()
    tgt_cp = pltpu.make_async_copy(tgt_in, tgt, loc_sem.at[6])
    tgt_cp.start()
    th_cp.wait()

    cut = (thr[...].astype(F32) + 0.5) / 2048.0
    zero = jnp.zeros_like(cut)
    cutb[0] = jnp.where(c == 0, jnp.concatenate([cut, zero], 1), jnp.concatenate([zero, cut], 1))

    barrier = pltpu.get_barrier_semaphore()
    peers = [dev(y, pmod(p + j), c, zh) for j in range(1, PLANE)]
    peers += [dev(ymod(y + j), p, c, zh) for j in range(1, ny)]
    peers += [dev(y, p, c, lmod(zh + j)) for j in range(1, nl)]
    peers += [partner]
    for peer in peers:
        pl.semaphore_signal(barrier, inc=1, device_id=peer, device_id_type=MESH)
    pl.semaphore_wait(barrier, len(peers))

    pending = []

    def plane_start(which, source, dest):
        out = []
        for j in range(1, PLANE):
            q = pmod(p + j)
            cp = remote(source(q), dest.at[p], pl_s.at[which, j - 1], pl_r.at[which, j - 1], dev(y, q, c, zh))
            cp.start()
            out.append(cp)
        pending.extend(out)
        return out

    def d2d_start(which, source, dest):
        cp = remote(source, dest, d2d_s.at[which], d2d_r.at[which], partner)
        cp.start()
        pending.append(cp)
        return cp

    def y_start(which, source, dest):
        out = []
        for j in range(1, ny):
            q = ymod(y + j)
            cp = remote(source(q), dest.at[y], ys_s.at[which, j - 1], ys_r.at[which, j - 1], dev(q, p, c, zh))
            cp.start()
            out.append(cp)
        pending.extend(out)
        return out

    def wait_all(copies):
        for cp in copies:
            cp.wait_recv()

    def repack(staged, tmp, n):
        for i in range(n):
            tmp[r * i : r * (i + 1), :] = staged[i].astype(F32)
        return tmp[...].astype(BF)

    def gather(which, first_a, first_b, in_a, in_b, buf, quilt):
        wait_all(first_a)
        buf[y, :, ca] = repack(in_a, tmp_a, PLANE)
        last_a = y_start(which + 1, lambda q: buf.at[y, :, ca], buf.at[:, :, ca])
        wait_all(first_b)
        quilt[p] = repack(in_b, tmp_b, ny)
        last_b = plane_start(which + 1, lambda q: quilt.at[p], quilt)
        wait_all(last_b)
        fixed = nn(perm[0], quilt[...].reshape(PLANE * rows_b, wb)).astype(BF)
        buf[:, :, cb] = fixed.reshape(ny, rows, wb)
        wait_all(last_a)

    first_b = y_start(0, lambda q: x_in.at[:, cb], st_b)
    first_a = plane_start(0, lambda q: x_in.at[:, ca], st_a)
    enc_d = d2d_start(0, enc_in, encb.at[c])
    cut_d = d2d_start(2, cutb.at[0], cutb.at[1])
    dec_d = d2d_start(1, dec_in, decb.at[:, c])
    xa_cp.wait()
    xb_cp.wait()
    perm_cp.wait()
    tgt_cp.wait()
    gather(0, first_a, first_b, st_a, st_b, xb, xq)
    x_d = d2d_start(4, xb, xp)

    enc_cp.wait()
    enc_d.wait_recv()
    cut_d.wait_recv()
    xv = xb[...].reshape(ny * rows, d)
    ev = encb[...].reshape(CORES * f, d)
    pa = nt(xv, ev)
    pre[...] = pa
    level = cutb[0] + cutb[1]
    act = jnp.where(pa > level, pa, 0.0).astype(BF)
    acts[zh] = act

    def layer_start(which, source, dest):
        out = []
        for j in range(1, nl):
            l = lmod(zh + j)
            cp = remote(source(l), dest.at[zh], lay_s.at[which, j - 1], lay_r.at[which, j - 1], dev(y, p, c, l))
            cp.start()
            out.append(cp)
        pending.extend(out)
        return out

    al = layer_start(0, lambda l: acts.at[zh], acts)
    msum[0] = jnp.sum(jnp.abs(act.astype(F32)), axis=0, keepdims=True)
    mag_d = d2d_start(3, msum.at[0], msum.at[1])
    dec_cp.wait()
    dec_d.wait_recv()
    for cp in al:
        cp.wait_recv()

    av = jnp.concatenate([acts[s] for s in range(nl)], axis=1)
    qv = nn(perm[1], av).astype(BF)
    dv = decb[...].reshape(nl * CORES * f, d)
    out_b = nn(qv, dv[:, wa:]).reshape(PLANE, rows_b, wb)
    part_b[...] = out_b
    rs_b[...] = out_b.astype(BF)
    down_b = plane_start(2, lambda q: rs_b.at[q], rr_b)
    out_a = nn(av, dv[:, :wa]).reshape(ny, rows, wa)
    part_a[...] = out_a
    rs_a[...] = out_a.astype(BF)
    down_a = y_start(2, lambda q: rs_a.at[q], rr_a)

    for s in range(nl):
        act_t[s] = jnp.transpose(acts[s].astype(F32)).astype(BF)
    act_d = d2d_start(5, act_t.at[:, pl.ds(pl.multiple_of((1 - c) * f, f), f)], act_o)

    wait_all(down_b)
    total = part_b[p]
    for j in range(1, PLANE):
        total = total + rr_b[pmod(p + j)].astype(F32)
    tmp_b[...] = total
    for i in range(ny):
        so_b[i] = tmp_b[r * i : r * (i + 1), :].astype(BF)
    own_b = y_start(3, lambda q: so_b.at[q], si_b)
    si_b[y] = so_b[y]
    wait_all(down_a)
    total = part_a[y]
    for j in range(1, ny):
        total = total + rr_a[ymod(y + j)].astype(F32)
    tmp_a[...] = total
    for i in range(PLANE):
        so_a[i] = tmp_a[r * i : r * (i + 1), :].astype(BF)
    own_a = plane_start(3, lambda q: so_a.at[q], si_a)
    si_a[p] = so_a[p]

    def added(slots, n):
        total = slots[0].astype(F32)
        for i in range(1, n):
            total = total + slots[i].astype(F32)
        return total

    wait_all(own_b)
    recon_b = added(si_b, ny)
    wait_all(own_a)
    recon_a = added(si_a, PLANE)
    recon = jnp.concatenate([recon_a, recon_b], axis=1)
    rec_out[...] = recon.astype(BF)
    error = recon - tgt[...].astype(F32)
    gown[...] = (error * (1.0 / ERROR_SCALE)).astype(BF)
    first_b = y_start(4, lambda q: gown.at[:, cb], gs_b)
    first_a = plane_start(4, lambda q: gown.at[:, ca], gs_a)
    gs_a[p] = gown[:, ca]
    gs_b[y] = gown[:, cb]
    mag_d.wait_recv()
    magnitude = (msum[0] + msum[1]) * (1.0 / tokens)
    penalty = jnp.sum(magnitude * magnitude)
    scalar = jnp.sum(error * error) + (2.0 * ERROR_SCALE * PENALTY_WEIGHT / CORES) * penalty
    sc_p[p] = jnp.full((1, 128), scalar, F32)
    scp = plane_start(6, lambda q: sc_p.at[p], sc_p)
    gather(4, first_a, first_b, gs_a, gs_b, gb, gq)
    g_d = d2d_start(6, gb, gp)

    gv = gb[...].reshape(ny * rows, d)
    agl = []
    for j in range(1, nl):
        l = lmod(zh + j)
        ags[j] = nt(gv, decb[l].reshape(CORES * f, d)).astype(BF)
        cp = remote(ags.at[j], agr.at[zh], lay_s.at[1, j - 1], lay_r.at[1, j - 1], dev(y, p, c, l))
        cp.start()
        agl.append(cp)
    pending.extend(agl)
    agf[...] = nt(gv, decb[zh].reshape(CORES * f, d))

    def fold(slots, n):
        total = slots[0]
        for i in range(1, n):
            total = total + slots[i]
        return total

    for cp in scp:
        cp.wait_recv()
    sc_y[y] = fold(sc_p, PLANE)
    scy = y_start(6, lambda q: sc_y.at[y], sc_y)

    act_d.wait_recv()
    g_d.wait_recv()
    go = gp[...].reshape(ny * rows, d)
    own = pl.ds(pl.multiple_of(c * f, f), f)
    lhs = jnp.concatenate([act_t[s, own, :] for s in range(nl)], axis=0)
    lho = jnp.concatenate([act_o[s] for s in range(nl)], axis=0)
    dg_out[...] = (nn(lhs, gv) + nn(lho, go)).astype(BF).reshape(nl, f, d)

    for cp in scy:
        cp.wait_recv()
    sc_l[zh] = fold(sc_y, ny)
    scl = layer_start(2, lambda l: sc_l.at[zh], sc_l)

    for cp in agl:
        cp.wait_recv()
    act_grad = agf[...]
    for j in range(1, nl):
        act_grad = act_grad + agr[lmod(zh + j)].astype(F32)
    pv = pre[...]
    fire = pv > level
    sign = jnp.where(fire & (pv > 0.0), 1.0, 0.0) - jnp.where(fire & (pv < 0.0), 1.0, 0.0)
    sparsity = (2.0 * PENALTY_WEIGHT) * magnitude * sign / float(tokens)
    pg = jnp.where(fire, act_grad + sparsity, 0.0)
    pgt[...] = jnp.transpose(pg).astype(BF)
    pg_d = d2d_start(7, pgt.at[pl.ds(pl.multiple_of((1 - c) * f, f), f)], pgo)
    for cp in scl:
        cp.wait_recv()
    sc_c[c] = fold(sc_l, nl)
    sc_d = d2d_start(8, sc_c.at[c], sc_c.at[c])
    x_d.wait_recv()
    eg = nn(pgt[own, :], xb[...].reshape(ny * rows, d))
    pg_d.wait_recv()
    eg = eg + nn(pgo[...], xp[...].reshape(ny * rows, d))
    eg_out[...] = eg.astype(BF)
    sc_d.wait_recv()
    loss_out[...] = fold(sc_c, CORES) * (1.0 / (nl * tokens * d))
    for cp in pending:
        cp.wait_send()


def emit(loss_in, rec_in, dg_in, eg_in, loss_out, rec_out, dg_out, eg_out, sem):
    pairs = ((dg_in, dg_out), (eg_in, eg_out), (rec_in, rec_out), (loss_in, loss_out))
    copies = [pltpu.make_async_copy(a, b, sem.at[i]) for i, (a, b) in enumerate(pairs)]
    for cp in copies:
        cp.start()
    for cp in copies:
        cp.wait()


def solution(mesh):
    nl = mesh.shape["layer"]
    ny = mesh.shape["feat"] // (PLANE * CORES)

    def body(residual_in, enc_weight, thresholds, dec_weight, target):
        r, d = residual_in.shape[1:]
        f = enc_weight.shape[2]
        rows = PLANE * r
        wa = d // PARTS
        wb = d - wa
        rows_b = ny * r
        t = ny * rows
        spot = np.arange(t).reshape(PLANE, ny, r).transpose(1, 0, 2).reshape(t)
        eye = np.eye(t, dtype=np.float32)
        perm = jnp.asarray(np.stack([eye[spot], eye[spot].T]), BF)
        any_spec = pl.BlockSpec(memory_space=pl.ANY)
        vm = pl.BlockSpec(memory_space=pltpu.VMEM)
        hbm = pl.BlockSpec(memory_space=pltpu.HBM)
        V = pltpu.VMEM
        dma = pltpu.SemaphoreType.DMA
        shapes = (
            jax.ShapeDtypeStruct((1, 128), F32),
            jax.ShapeDtypeStruct((r, d), BF),
            jax.ShapeDtypeStruct((nl, f, d), BF),
            jax.ShapeDtypeStruct((f, d), BF),
        )
        results = pl.pallas_call(
            functools.partial(kernel, (ny, nl, r, d, f)),
            out_shape=shapes,
            in_specs=[hbm] * 6,
            out_specs=(vm, vm, vm, vm),
            scratch_shapes=[
                V((PLANE, r, wa), BF), V((ny, r, wb), BF), V((PLANE, r, wa), BF), V((ny, r, wb), BF),
                V((r, d), BF), V((rows, wa), F32), V((rows_b, wb), F32),
                V((ny, rows, d), BF), V((ny, rows, d), BF), V((ny, rows, d), BF), V((ny, rows, d), BF),
                V((PLANE, rows_b, wb), BF), V((PLANE, rows_b, wb), BF),
                V((1, f), jnp.int32), V((r, d), BF),
                V((CORES, f, d), BF), V((nl, CORES, f, d), BF), V((2, 1, CORES * f), F32), V((2, 1, CORES * f), F32),
                V((t, CORES * f), F32), V((nl, t, CORES * f), BF), V((nl, CORES * f, t), BF), V((nl, f, t), BF), V((2, t, t), BF),
                V((ny, rows, wa), F32), V((PLANE, rows_b, wb), F32),
                V((ny, rows, wa), BF), V((PLANE, rows_b, wb), BF), V((ny, rows, wa), BF), V((PLANE, rows_b, wb), BF),
                V((PLANE, r, wa), BF), V((ny, r, wb), BF), V((PLANE, r, wa), BF), V((ny, r, wb), BF),
                V((t, CORES * f), F32), V((nl, t, CORES * f), BF), V((nl, t, CORES * f), BF),
                V((CORES * f, t), BF), V((f, t), BF),
                V((PLANE, 1, 128), F32), V((ny, 1, 128), F32), V((nl, 1, 128), F32), V((CORES, 1, 128), F32),
                dma((7,)), dma((9,)), dma((9,)), dma((7, PLANE - 1)), dma((7, PLANE - 1)),
                dma((7, ny - 1)), dma((7, ny - 1)), dma((3, nl - 1)), dma((3, nl - 1)),
            ],
            compiler_params=pltpu.CompilerParams(
                collective_id=0, has_side_effects=True, vmem_limit_bytes=32 * 1024 * 1024
            ),
            name="step",
        )(
            *(
                pltpu.with_memory_space_constraint(v, pltpu.HBM)
                for v in (
                    residual_in[0],
                    jnp.swapaxes(enc_weight[0], 0, 1),
                    thresholds,
                    dec_weight[:, 0],
                    target[0],
                    perm,
                )
            )
        )
        loss, rec, dg, eg = pl.pallas_call(
            emit,
            out_shape=shapes,
            in_specs=[any_spec] * 4,
            out_specs=[hbm] * 4,
            scratch_shapes=[dma((4,))],
            compiler_params=pltpu.CompilerParams(vmem_limit_bytes=1024 * 1024),
            name="emit",
        )(*results)
        return loss[0, 0], rec[None], dg[:, None], jnp.swapaxes(eg, 0, 1)[None]

    return jax.shard_map(
        body,
        mesh=mesh,
        in_specs=(
            P("layer", "feat", None),
            P("layer", None, "feat"),
            P("layer", "feat"),
            P(None, "layer", "feat", None),
            P("layer", "feat", None),
        ),
        out_specs=(
            P(),
            P("layer", "feat", None),
            P(None, "layer", "feat", None),
            P("layer", None, "feat"),
        ),
        check_vma=False,
    )
```

```python
import functools

import jax
import jax.numpy as jnp
import numpy as np
from jax import lax
from jax.experimental import pallas as pl
from jax.experimental.pallas import tpu as pltpu
from jax.sharding import PartitionSpec as P

ERROR_SCALE = 32.0
PENALTY_WEIGHT = 4.0
MESH = pl.DeviceIdType.MESH
PLANE = 8
CORES = 2
PARTS = 3
BF = jnp.bfloat16
F32 = jnp.float32


def nt(a, b):
    return lax.dot_general(a, b, (((1,), (1,)), ((), ())), preferred_element_type=F32)


def nn(a, b):
    return lax.dot_general(a, b, (((1,), (0,)), ((), ())), preferred_element_type=F32)


def kernel(
    dims,
    x_in, enc_in, th_in, dec_in, tgt_in, perm_in,
    loss_out, rec_out, dg_out, eg_out,
    st_a, st_b, gs_a, gs_b, gown, tmp_a, tmp_b, xb, gb, xp, gp, xq, gq,
    thr, tgt, encb, decb, cutb, msum, pre, acts, act_t, act_o, perm,
    part_a, part_b, rs_a, rs_b, rr_a, rr_b, so_a, so_b, si_a, si_b,
    agf, ags, agr, pgt, pgo,
    sc_p, sc_y, sc_l, sc_c,
    loc_sem, d2d_s, d2d_r, pl_s, pl_r, ys_s, ys_r, lay_s, lay_r,
):
    ny, nl, r, d, f = dims
    wa = d // PARTS
    wb = d - wa
    ca, cb = pl.ds(0, wa), pl.ds(wa, wb)
    rows = PLANE * r
    rows_b = ny * r
    tokens = ny * rows * CORES
    feat = lax.axis_index("feat")
    zh = lax.axis_index("layer")
    c = lax.rem(feat, CORES)
    p = lax.rem(feat // CORES, PLANE)
    y = feat // (CORES * PLANE)

    def dev(yy, pp, cc, ll):
        return (yy * (PLANE * CORES) + pp * CORES + cc, ll)

    def ymod(v):
        return lax.rem(v + 2 * ny, ny)

    def pmod(v):
        return lax.rem(v + PLANE, PLANE)

    def lmod(v):
        return lax.rem(v + nl, nl)

    def remote(src, dst, ss, rs, device):
        return pltpu.make_async_remote_copy(
            src_ref=src, dst_ref=dst, send_sem=ss, recv_sem=rs, device_id=device, device_id_type=MESH
        )

    partner = dev(y, p, 1 - c, zh)

    enc_cp = pltpu.make_async_copy(enc_in, encb.at[c], loc_sem.at[0])
    enc_cp.start()
    dec_cp = pltpu.make_async_copy(dec_in, decb.at[:, c], loc_sem.at[1])
    dec_cp.start()
    xa_cp = pltpu.make_async_copy(x_in.at[:, ca], st_a.at[p], loc_sem.at[2])
    xa_cp.start()
    xb_cp = pltpu.make_async_copy(x_in.at[:, cb], st_b.at[y], loc_sem.at[3])
    xb_cp.start()
    perm_cp = pltpu.make_async_copy(perm_in, perm, loc_sem.at[4])
    perm_cp.start()
    th_cp = pltpu.make_async_copy(th_in, thr, loc_sem.at[5])
    th_cp.start()
    tgt_cp = pltpu.make_async_copy(tgt_in, tgt, loc_sem.at[6])
    tgt_cp.start()
    th_cp.wait()

    cut = (thr[...].astype(F32) + 0.5) / 2048.0
    zero = jnp.zeros_like(cut)
    cutb[0] = jnp.where(c == 0, jnp.concatenate([cut, zero], 1), jnp.concatenate([zero, cut], 1))

    barrier = pltpu.get_barrier_semaphore()
    peers = [dev(y, pmod(p + j), c, zh) for j in range(1, PLANE)]
    peers += [dev(ymod(y + j), p, c, zh) for j in range(1, ny)]
    peers += [dev(y, p, c, lmod(zh + j)) for j in range(1, nl)]
    peers += [partner]
    for peer in peers:
        pl.semaphore_signal(barrier, inc=1, device_id=peer, device_id_type=MESH)
    pl.semaphore_wait(barrier, len(peers))

    pending = []

    def plane_start(which, source, dest):
        out = []
        for j in range(1, PLANE):
            q = pmod(p + j)
            cp = remote(source(q), dest.at[p], pl_s.at[which, j - 1], pl_r.at[which, j - 1], dev(y, q, c, zh))
            cp.start()
            out.append(cp)
        pending.extend(out)
        return out

    def d2d_start(which, source, dest):
        cp = remote(source, dest, d2d_s.at[which], d2d_r.at[which], partner)
        cp.start()
        pending.append(cp)
        return cp

    def y_start(which, source, dest):
        out = []
        for j in range(1, ny):
            q = ymod(y + j)
            cp = remote(source(q), dest.at[y], ys_s.at[which, j - 1], ys_r.at[which, j - 1], dev(q, p, c, zh))
            cp.start()
            out.append(cp)
        pending.extend(out)
        return out

    def wait_all(copies):
        for cp in copies:
            cp.wait_recv()

    def repack(staged, tmp, n):
        for i in range(n):
            tmp[r * i : r * (i + 1), :] = staged[i].astype(F32)
        return tmp[...].astype(BF)

    def gather(which, first_a, first_b, in_a, in_b, buf, quilt, between=None):
        wait_all(first_a)
        buf[y, :, ca] = repack(in_a, tmp_a, PLANE)
        last_a = y_start(which + 1, lambda q: buf.at[y, :, ca], buf.at[:, :, ca])
        wait_all(first_b)
        quilt[p] = repack(in_b, tmp_b, ny)
        last_b = plane_start(which + 1, lambda q: quilt.at[p], quilt)
        if between is not None:
            between()
        wait_all(last_b)
        fixed = nn(perm[0], quilt[...].reshape(PLANE * rows_b, wb)).astype(BF)
        buf[:, :, cb] = fixed.reshape(ny, rows, wb)
        wait_all(last_a)

    first_b = y_start(0, lambda q: x_in.at[:, cb], st_b)
    first_a = plane_start(0, lambda q: x_in.at[:, ca], st_a)
    enc_d = d2d_start(0, enc_in, encb.at[c])
    cut_d = d2d_start(2, cutb.at[0], cutb.at[1])
    dec_d = d2d_start(1, dec_in, decb.at[:, c])
    xa_cp.wait()
    xb_cp.wait()
    perm_cp.wait()
    tgt_cp.wait()
    gather(0, first_a, first_b, st_a, st_b, xb, xq)
    x_d = d2d_start(4, xb, xp)

    enc_cp.wait()
    enc_d.wait_recv()
    cut_d.wait_recv()
    xv = xb[...].reshape(ny * rows, d)
    ev = encb[...].reshape(CORES * f, d)
    pa = nt(xv, ev)
    pre[...] = pa
    level = cutb[0] + cutb[1]
    act = jnp.where(pa > level, pa, 0.0).astype(BF)
    acts[zh] = act

    def layer_start(which, source, dest):
        out = []
        for j in range(1, nl):
            l = lmod(zh + j)
            cp = remote(source(l), dest.at[zh], lay_s.at[which, j - 1], lay_r.at[which, j - 1], dev(y, p, c, l))
            cp.start()
            out.append(cp)
        pending.extend(out)
        return out

    al = layer_start(0, lambda l: acts.at[zh], acts)
    msum[0] = jnp.sum(jnp.abs(act.astype(F32)), axis=0, keepdims=True)
    mag_d = d2d_start(3, msum.at[0], msum.at[1])
    dec_cp.wait()
    dec_d.wait_recv()
    for cp in al:
        cp.wait_recv()

    av = jnp.concatenate([acts[s] for s in range(nl)], axis=1)
    qv = nn(perm[1], av).astype(BF)
    dv = decb[...].reshape(nl * CORES * f, d)
    out_b = nn(qv, dv[:, wa:]).reshape(PLANE, rows_b, wb)
    part_b[...] = out_b
    rs_b[...] = out_b.astype(BF)
    down_b = plane_start(2, lambda q: rs_b.at[q], rr_b)
    out_a = nn(av, dv[:, :wa]).reshape(ny, rows, wa)
    part_a[...] = out_a
    rs_a[...] = out_a.astype(BF)
    down_a = y_start(2, lambda q: rs_a.at[q], rr_a)

    for s in range(nl):
        act_t[s] = jnp.transpose(acts[s].astype(F32)).astype(BF)
    act_d = d2d_start(5, act_t.at[:, pl.ds(pl.multiple_of((1 - c) * f, f), f)], act_o)

    wait_all(down_b)
    total = part_b[p]
    for j in range(1, PLANE):
        total = total + rr_b[pmod(p + j)].astype(F32)
    tmp_b[...] = total
    for i in range(ny):
        so_b[i] = tmp_b[r * i : r * (i + 1), :].astype(BF)
    own_b = y_start(3, lambda q: so_b.at[q], si_b)
    si_b[y] = so_b[y]
    wait_all(down_a)
    total = part_a[y]
    for j in range(1, ny):
        total = total + rr_a[ymod(y + j)].astype(F32)
    tmp_a[...] = total
    for i in range(PLANE):
        so_a[i] = tmp_a[r * i : r * (i + 1), :].astype(BF)
    own_a = plane_start(3, lambda q: so_a.at[q], si_a)
    si_a[p] = so_a[p]

    def added(slots, n):
        total = slots[0].astype(F32)
        for i in range(1, n):
            total = total + slots[i].astype(F32)
        return total

    wait_all(own_b)
    recon_b = added(si_b, ny)
    wait_all(own_a)
    recon_a = added(si_a, PLANE)
    recon = jnp.concatenate([recon_a, recon_b], axis=1)
    rec_out[...] = recon.astype(BF)
    error = recon - tgt[...].astype(F32)
    gown[...] = (error * (1.0 / ERROR_SCALE)).astype(BF)
    first_b = y_start(4, lambda q: gown.at[:, cb], gs_b)
    first_a = plane_start(4, lambda q: gown.at[:, ca], gs_a)
    gs_a[p] = gown[:, ca]
    gs_b[y] = gown[:, cb]
    mag_d.wait_recv()
    magnitude = (msum[0] + msum[1]) * (1.0 / tokens)
    penalty = jnp.sum(magnitude * magnitude)
    scalar = jnp.sum(error * error) + (2.0 * ERROR_SCALE * PENALTY_WEIGHT / CORES) * penalty
    sc_p[p] = jnp.full((1, 128), scalar, F32)
    scp = plane_start(6, lambda q: sc_p.at[p], sc_p)
    def fold(slots, n):
        total = slots[0]
        for i in range(1, n):
            total = total + slots[i]
        return total

    scy = []

    def scalar_y():
        wait_all(scp)
        sc_y[y] = fold(sc_p, PLANE)
        scy.extend(y_start(6, lambda q: sc_y.at[y], sc_y))

    gather(4, first_a, first_b, gs_a, gs_b, gb, gq, scalar_y)
    g_d = d2d_start(6, gb, gp)

    gv = gb[...].reshape(ny * rows, d)
    agl = []
    for j in range(1, nl):
        l = lmod(zh + j)
        ags[j] = nt(gv, decb[l].reshape(CORES * f, d)).astype(BF)
        cp = remote(ags.at[j], agr.at[zh], lay_s.at[1, j - 1], lay_r.at[1, j - 1], dev(y, p, c, l))
        cp.start()
        agl.append(cp)
    pending.extend(agl)
    wait_all(scy)
    sc_l[zh] = fold(sc_y, ny)
    scl = layer_start(2, lambda l: sc_l.at[zh], sc_l)
    agf[...] = nt(gv, decb[zh].reshape(CORES * f, d))

    act_d.wait_recv()
    g_d.wait_recv()
    go = gp[...].reshape(ny * rows, d)
    own = pl.ds(pl.multiple_of(c * f, f), f)
    lhs = jnp.concatenate([act_t[s, own, :] for s in range(nl)], axis=0)
    lho = jnp.concatenate([act_o[s] for s in range(nl)], axis=0)
    dg_out[...] = (nn(lhs, gv) + nn(lho, go)).astype(BF).reshape(nl, f, d)

    for cp in scl:
        cp.wait_recv()
    sc_c[c] = fold(sc_l, nl)
    sc_d = d2d_start(8, sc_c.at[c], sc_c.at[c])

    for cp in agl:
        cp.wait_recv()
    act_grad = agf[...]
    for j in range(1, nl):
        act_grad = act_grad + agr[lmod(zh + j)].astype(F32)
    pv = pre[...]
    fire = pv > level
    sign = jnp.where(fire & (pv > 0.0), 1.0, 0.0) - jnp.where(fire & (pv < 0.0), 1.0, 0.0)
    sparsity = (2.0 * PENALTY_WEIGHT) * magnitude * sign / float(tokens)
    pg = jnp.where(fire, act_grad + sparsity, 0.0)
    pgt[...] = jnp.transpose(pg).astype(BF)
    pg_d = d2d_start(7, pgt.at[pl.ds(pl.multiple_of((1 - c) * f, f), f)], pgo)
    x_d.wait_recv()
    eg = nn(pgt[own, :], xb[...].reshape(ny * rows, d))
    pg_d.wait_recv()
    eg = eg + nn(pgo[...], xp[...].reshape(ny * rows, d))
    eg_out[...] = eg.astype(BF)
    sc_d.wait_recv()
    loss_out[...] = fold(sc_c, CORES) * (1.0 / (nl * tokens * d))
    for cp in pending:
        cp.wait_send()


def emit(loss_in, rec_in, dg_in, eg_in, loss_out, rec_out, dg_out, eg_out, sem):
    pairs = ((dg_in, dg_out), (eg_in, eg_out), (rec_in, rec_out), (loss_in, loss_out))
    copies = [pltpu.make_async_copy(a, b, sem.at[i]) for i, (a, b) in enumerate(pairs)]
    for cp in copies:
        cp.start()
    for cp in copies:
        cp.wait()


def solution(mesh):
    nl = mesh.shape["layer"]
    ny = mesh.shape["feat"] // (PLANE * CORES)

    def body(residual_in, enc_weight, thresholds, dec_weight, target):
        r, d = residual_in.shape[1:]
        f = enc_weight.shape[2]
        rows = PLANE * r
        wa = d // PARTS
        wb = d - wa
        rows_b = ny * r
        t = ny * rows
        spot = np.arange(t).reshape(PLANE, ny, r).transpose(1, 0, 2).reshape(t)
        eye = np.eye(t, dtype=np.float32)
        perm = jnp.asarray(np.stack([eye[spot], eye[spot].T]), BF)
        any_spec = pl.BlockSpec(memory_space=pl.ANY)
        vm = pl.BlockSpec(memory_space=pltpu.VMEM)
        hbm = pl.BlockSpec(memory_space=pltpu.HBM)
        V = pltpu.VMEM
        dma = pltpu.SemaphoreType.DMA
        shapes = (
            jax.ShapeDtypeStruct((1, 128), F32),
            jax.ShapeDtypeStruct((r, d), BF),
            jax.ShapeDtypeStruct((nl, f, d), BF),
            jax.ShapeDtypeStruct((f, d), BF),
        )
        results = pl.pallas_call(
            functools.partial(kernel, (ny, nl, r, d, f)),
            out_shape=shapes,
            in_specs=[hbm] * 6,
            out_specs=(vm, vm, vm, vm),
            scratch_shapes=[
                V((PLANE, r, wa), BF), V((ny, r, wb), BF), V((PLANE, r, wa), BF), V((ny, r, wb), BF),
                V((r, d), BF), V((rows, wa), F32), V((rows_b, wb), F32),
                V((ny, rows, d), BF), V((ny, rows, d), BF), V((ny, rows, d), BF), V((ny, rows, d), BF),
                V((PLANE, rows_b, wb), BF), V((PLANE, rows_b, wb), BF),
                V((1, f), jnp.int32), V((r, d), BF),
                V((CORES, f, d), BF), V((nl, CORES, f, d), BF), V((2, 1, CORES * f), F32), V((2, 1, CORES * f), F32),
                V((t, CORES * f), F32), V((nl, t, CORES * f), BF), V((nl, CORES * f, t), BF), V((nl, f, t), BF), V((2, t, t), BF),
                V((ny, rows, wa), F32), V((PLANE, rows_b, wb), F32),
                V((ny, rows, wa), BF), V((PLANE, rows_b, wb), BF), V((ny, rows, wa), BF), V((PLANE, rows_b, wb), BF),
                V((PLANE, r, wa), BF), V((ny, r, wb), BF), V((PLANE, r, wa), BF), V((ny, r, wb), BF),
                V((t, CORES * f), F32), V((nl, t, CORES * f), BF), V((nl, t, CORES * f), BF),
                V((CORES * f, t), BF), V((f, t), BF),
                V((PLANE, 1, 128), F32), V((ny, 1, 128), F32), V((nl, 1, 128), F32), V((CORES, 1, 128), F32),
                dma((7,)), dma((9,)), dma((9,)), dma((7, PLANE - 1)), dma((7, PLANE - 1)),
                dma((7, ny - 1)), dma((7, ny - 1)), dma((3, nl - 1)), dma((3, nl - 1)),
            ],
            compiler_params=pltpu.CompilerParams(
                collective_id=0, has_side_effects=True, vmem_limit_bytes=32 * 1024 * 1024
            ),
            name="step",
        )(
            *(
                pltpu.with_memory_space_constraint(v, pltpu.HBM)
                for v in (
                    residual_in[0],
                    jnp.swapaxes(enc_weight[0], 0, 1),
                    thresholds,
                    dec_weight[:, 0],
                    target[0],
                    perm,
                )
            )
        )
        loss, rec, dg, eg = pl.pallas_call(
            emit,
            out_shape=shapes,
            in_specs=[any_spec] * 4,
            out_specs=[hbm] * 4,
            scratch_shapes=[dma((4,))],
            compiler_params=pltpu.CompilerParams(vmem_limit_bytes=1024 * 1024),
            name="emit",
        )(*results)
        return loss[0, 0], rec[None], dg[:, None], jnp.swapaxes(eg, 0, 1)[None]

    return jax.shard_map(
        body,
        mesh=mesh,
        in_specs=(
            P("layer", "feat", None),
            P("layer", None, "feat"),
            P("layer", "feat"),
            P(None, "layer", "feat", None),
            P("layer", "feat", None),
        ),
        out_specs=(
            P(),
            P("layer", "feat", None),
            P(None, "layer", "feat", None),
            P("layer", None, "feat"),
        ),
        check_vma=False,
    )
```
